32 devices in a mesh: tm: 4 (over y, x), slab: 8 (over z, core).
Axes of the slice: x: 2, y: 2, z: 4, core: 2. Of those that a mesh axis runs over, the one named last changes fastest.
Arguments:
- increments: float32 [4, 768, 8, 768], P('tm', 'slab'), may hold values from -6 to 6
- courant: float32 [4, 768, 2, 768], P('tm', 'slab'), may hold values from -0.4 to 0.4
- deviation: float32 [768, 8, 768], P('slab'), may hold values from 0.5 to 2
- spectrum: float32 [768, 768], P(None, 'slab'), may hold values from 0.02 to 1
- observed_cells: int32 [4, 65536], P('tm', 'slab'), may hold values from 0 to 589823
- innovation: float32 [4, 65536], P('tm', 'slab'), may hold values from -6 to 6
- error_weights: float32 [4, 65536], P('tm', 'slab'), may hold values from 0.5 to 4
Outputs:
- gradient: float32 [4, 768, 8, 768], P('tm', 'slab')
The draws below stay inside these ranges and needn't reach their ends.
Inputs may be any that keep to these rules, and one draw needn't show every extreme that they name: `observed_cells`: entry s * 8192 + o of a subwindow's row indexes a cell of latitude slab s, numbered row-major over (row in the slab, vertical value, column); a cell may be observed more than once.
All inputs are finite; a program needn't handle non-finite values.
Results may differ from the reference program's by a relative error of at most 0.00005.
Values sent between devices are 32-bit elements; how exact they have to be, the bound alone decides.
A program may use at most 64 MiB of HBM per device.

```python
import math
import jax
import jax.numpy as jnp
from jax import lax

VERT = 8
LAT = 768
LON = 768
STEPS = 4
OBS_DEV = 8192
SUBW = 4
N_SLAB = 8


def place_ends(drawn, stream_key, smallest, top_value):
    dims = drawn.shape
    spot = [jax.random.randint(jax.random.fold_in(stream_key, axis), (), 0, dims[axis]) for axis in range(len(dims))]
    drawn = drawn.at[tuple(spot)].set(smallest)
    longest = dims.index(max(dims))
    spot[longest] = (spot[longest] + 1) % dims[longest]
    return drawn.at[tuple(spot)].set(top_value)


def steps_of(key, shape, cuts, least, high):
    gain, own = 1.0, jax.random.fold_in(key, 6)
    for axis_at, blocks in cuts:
        heights = jnp.exp(jax.random.uniform(jax.random.fold_in(own, axis_at), (blocks,), jnp.float32, least / len(cuts), high / len(cuts)))
        gain = gain * jnp.repeat(heights, shape[axis_at] // blocks).reshape([-1 if axis == axis_at else 1 for axis in range(len(shape))])
    return gain


def normal_values(key, shape, scale, limit, shards=(), kind=jnp.bfloat16):
    result = scale * jax.random.normal(key, shape, jnp.float32)
    if shards:
        result = result * steps_of(key, shape, shards, -0.22, 0.18)
    return jnp.clip(result, -limit, limit).astype(kind)


def setup_inputs(seed: int = 0) -> dict:
    key_list = jax.random.split(jax.random.key(seed), 8)
    return {
        "increments": normal_values(key_list[0], (SUBW, LAT, VERT, LON), 1.0, 6.0, ((0, 4), (1, 8)), jnp.float32),
        "courant": jnp.clip(jax.random.uniform(key_list[1], (SUBW, LAT, 2, LON), jnp.float32, -0.4, 0.4) * steps_of(key_list[1], (SUBW, LAT, 2, LON), ((0, 4), (1, 8)), -0.4, 0.0), -0.4, 0.4),
        "deviation": jnp.clip(jnp.exp(math.log(2.0) - 1.3862944 * jax.random.uniform(key_list[2], (LAT, VERT, LON), jnp.float32) ** steps_of(key_list[2], (LAT, VERT, LON), ((0, 8),), -0.2, 0.2)), 0.5, 2.0),
        "spectrum": jnp.clip(jnp.exp(math.log(1.0) - 3.912023 * jax.random.uniform(key_list[3], (LAT, LON), jnp.float32) ** steps_of(key_list[3], (LAT, LON), ((1, 8),), -0.2, 0.2)), 0.02, 1.0),
        "observed_cells": place_ends(jax.random.randint(key_list[4], (SUBW, N_SLAB * OBS_DEV), 0, (LAT // N_SLAB) * VERT * LON), jax.random.fold_in(key_list[4], 1), 0, ((LAT // N_SLAB) * VERT * LON) - 1).astype(jnp.int32),
        "innovation": normal_values(key_list[5], (SUBW, N_SLAB * OBS_DEV), 1.0, 6.0, ((0, 4), (1, 8)), jnp.float32),
        "error_weights": jnp.clip(jnp.exp(math.log(4.0) - 2.0794415 * jax.random.uniform(key_list[6], (SUBW, N_SLAB * OBS_DEV), jnp.float32) ** steps_of(key_list[6], (SUBW, N_SLAB * OBS_DEV), ((0, 4), (1, 8)), -0.2, 0.2)), 0.5, 4.0),
    }


DIFFUSION = 0.1
PRECISE = lax.Precision.HIGHEST

def hartley_table(length):
    index = jnp.arange(length, dtype=jnp.int32)
    phase = index[:, None] * index[None, :] % length
    angle = phase.astype(jnp.float32) * (2.0 * math.pi / length)
    return ((jnp.cos(angle) + jnp.sin(angle)) / math.sqrt(length)).astype(jnp.float32)

def cosine_table(length):
    index = jnp.arange(length, dtype=jnp.int32)
    phase = (2 * index[None, :] + 1) * index[:, None] % (4 * length)
    angle = phase.astype(jnp.float32) * (math.pi / (2 * length))
    scales = jnp.where(index == 0, math.sqrt(1.0 / length), math.sqrt(2.0 / length)).astype(jnp.float32)
    return (scales[:, None] * jnp.cos(angle)).astype(jnp.float32)

def tangent_step(state, winds):
    eastern = jnp.roll(state, -1, axis=2)
    western = jnp.roll(state, 1, axis=2)
    padded = jnp.pad(state, ((1, 1), (0, 0), (0, 0)))
    northern = padded[2:]
    southern = padded[:-2]
    zonal = winds[:, 0:1, :]
    meridional = winds[:, 1:2, :]
    spread = DIFFUSION * (northern + southern + eastern + western - 4.0 * state)
    return state + spread - 0.5 * zonal * (eastern - western) - 0.5 * meridional * (northern - southern)

def reference(increments, courant, deviation, spectrum, observed_cells, innovation, error_weights):

    def observe(state, cells):
        flat = state.reshape(N_SLAB, -1)
        return jnp.take_along_axis(flat, cells.reshape(N_SLAB, -1), axis=1).reshape(-1)

    def trajectory(forcing):

        def advance(carry, inputs):
            state = carry + inputs[0]
            for step_index in range(STEPS):
                state = tangent_step(state, inputs[1])
            return (state, observe(state, inputs[2]))
        final, seen = lax.scan(advance, jnp.zeros_like(forcing[0]), (forcing, courant, observed_cells))
        return seen
    seen, pullback = jax.vjp(trajectory, increments)
    adjoint, = pullback(error_weights * (seen - innovation))
    zonal_table = hartley_table(LON)
    merid_table = cosine_table(LAT)

    def covariance(field):
        scaled = deviation * field
        zonal = jnp.dot(scaled.reshape(-1, LON), zonal_table, preferred_element_type=jnp.float32, precision=PRECISE)
        merid = jnp.dot(merid_table, zonal.reshape(LAT, -1), preferred_element_type=jnp.float32, precision=PRECISE)
        merid = merid.reshape(LAT, VERT, LON) * spectrum[:, None, :]
        back = jnp.dot(merid_table.T, merid.reshape(LAT, -1), preferred_element_type=jnp.float32, precision=PRECISE)
        zonal_back = jnp.dot(back.reshape(-1, LON), zonal_table, preferred_element_type=jnp.float32, precision=PRECISE)
        return deviation * zonal_back.reshape(LAT, VERT, LON)
    return increments + lax.map(covariance, adjoint)
```

```python
import functools
import math

import jax
import jax.numpy as jnp
from jax import lax
from jax.experimental import pallas as pl
from jax.experimental.pallas import tpu as pltpu
from jax.sharding import PartitionSpec as P

LEVELS = 2
STEPS = 4


DIFFUSION = 0.1
PRECISE = lax.Precision.HIGHEST


def with_halo(cells, sides, width):
    for axis, dim in sides:
        count = lax.axis_size(axis)
        ends = count - 1
        head = lax.slice_in_dim(cells, 0, width, axis=dim)
        tail = lax.slice_in_dim(cells, cells.shape[dim] - width, cells.shape[dim], axis=dim)
        cells = jnp.concatenate(
            [
                lax.ppermute(tail, axis, [(i, (i + 1) % count) for i in range(ends)]),
                cells,
                lax.ppermute(head, axis, [((i + 1) % count, i) for i in range(ends)]),
            ],
            axis=dim,
        )
    return cells


def from_behind(value, axis, steps):
    count = lax.axis_size(axis)
    first, last = (max(0, -steps), min(count, count - steps))
    return lax.ppermute(value, axis, [(source, source + steps) for source in range(first, last)])


def hartley_table(length):
    index = jnp.arange(length, dtype=jnp.int32)
    phase = index[:, None] * index[None, :] % length
    angle = phase.astype(jnp.float32) * (2.0 * math.pi / length)
    return (jnp.cos(angle) + jnp.sin(angle)) / math.sqrt(length)


def cosine_table(length):
    index = jnp.arange(length, dtype=jnp.int32)
    phase = (2 * index[None, :] + 1) * index[:, None] % (4 * length)
    angle = phase.astype(jnp.float32) * (math.pi / (2 * length))
    scales = jnp.where(index == 0, math.sqrt(1.0 / length), math.sqrt(2.0 / length)).astype(
        jnp.float32
    )
    return scales[:, None] * jnp.cos(angle)


def rims(values):
    return with_halo(values, (("slab", 0),), STEPS)


def forward_sweep(current, winds, inside):
    for step_index in range(STEPS):
        height = current.shape[0]
        lower = step_index + 1
        upper = lower + height - 2
        centre = current[1:-1]
        northern = current[2:]
        southern = current[:-2]
        eastern = jnp.roll(centre, -1, axis=2)
        western = jnp.roll(centre, 1, axis=2)
        local_winds = winds[lower:upper]
        zonal = local_winds[:, 0:1, :]
        meridional = local_winds[:, 1:2, :]
        spread = DIFFUSION * (northern + southern + eastern + western - 4.0 * centre)
        updated = (
            centre
            + spread
            - 0.5 * zonal * (eastern - western)
            - 0.5 * meridional * (northern - southern)
        )
        current = updated * inside[lower:upper]
    return current


def adjoint_sweep(current, winds, inside):
    for step_index in range(STEPS):
        height = current.shape[0]
        local_winds = winds[step_index : step_index + height]
        zonal_flux = local_winds[:, 0:1, :] * current
        merid_flux = local_winds[:, 1:2, :] * current
        centre = current[1:-1]
        northern = current[2:]
        southern = current[:-2]
        eastern = jnp.roll(centre, -1, axis=2)
        western = jnp.roll(centre, 1, axis=2)
        zonal_centre = zonal_flux[1:-1]
        spread = DIFFUSION * (northern + southern + eastern + western - 4.0 * centre)
        carried = 0.5 * (jnp.roll(zonal_centre, -1, axis=2) - jnp.roll(zonal_centre, 1, axis=2))
        carried = carried + 0.5 * (merid_flux[2:] - merid_flux[:-2])
        lower = step_index + 1
        current = (centre + spread + carried) * inside[lower : lower + height - 2]
    return current


def body(*arrays):
    row_count, vertical, columns = arrays[0].shape[1:]
    if transposed_fits(lax.axis_size("tm"), lax.axis_size("slab"), row_count, vertical, columns, arrays[4].shape[1]):
        return transposed_body(*arrays)
    return pipelined_body(*arrays)


def pipelined_body(increments, courant, deviation, spectrum, observed_cells, innovation, error_weights):
    state_now = increments[0]
    row_count, vertical, columns = state_now.shape
    chain_len = lax.axis_size("tm")
    position = lax.axis_index("tm")
    total_rows = spectrum.shape[0]
    first_row = lax.axis_index("slab") * row_count - STEPS
    global_rows = first_row + jnp.arange(row_count + 2 * STEPS, dtype=jnp.int32)
    inside = ((global_rows >= 0) & (global_rows < total_rows)).astype(jnp.float32)[:, None, None]
    winds = rims(courant[0])
    block_width = 2 * LEVELS
    block_count = vertical // block_width
    ticks = chain_len + block_count - 1
    empty_block = jnp.zeros((row_count, block_width, columns), jnp.float32)

    def forward_tick(tick, carry):
        arriving, ends = carry
        block = tick - position
        valid = (block >= 0) & (block < block_count)
        offset = jnp.clip(block, 0, block_count - 1) * block_width
        start = arriving + lax.dynamic_slice_in_dim(state_now, offset, block_width, 1)
        finish = forward_sweep(rims(start), winds, inside)
        ends = jnp.where(valid, lax.dynamic_update_slice_in_dim(ends, finish, offset, 1), ends)
        arriving = from_behind(finish, "tm", 1)
        return (arriving, ends)

    arrived, ends = lax.fori_loop(0, ticks, forward_tick, (empty_block, jnp.zeros_like(state_now)))
    cells = observed_cells[0]
    seen = ends.reshape(-1)[cells]
    misfit = error_weights[0] * (seen - innovation[0])
    forcing = jnp.zeros((row_count * vertical * columns,), jnp.float32).at[cells].add(misfit)
    forcing = forcing.reshape(row_count, vertical, columns)

    def backward_tick(tick, carry):
        arriving, starts = carry
        block = tick - (chain_len - 1 - position)
        valid = (block >= 0) & (block < block_count)
        offset = jnp.clip(block, 0, block_count - 1) * block_width
        ending = arriving + lax.dynamic_slice_in_dim(forcing, offset, block_width, 1)
        begun = adjoint_sweep(rims(ending), winds, inside)
        starts = jnp.where(valid, lax.dynamic_update_slice_in_dim(starts, begun, offset, 1), starts)
        arriving = from_behind(begun, "tm", -1)
        return (arriving, starts)

    returned, adjoint = lax.fori_loop(
        0, ticks, backward_tick, (empty_block, jnp.zeros_like(state_now))
    )
    zonal_table = hartley_table(columns)
    merid_table = cosine_table(total_rows)
    scaled = deviation * adjoint
    zonal = jnp.dot(
        scaled.reshape(-1, columns),
        zonal_table,
        preferred_element_type=jnp.float32,
        precision=PRECISE,
    )
    zonal = zonal.reshape(row_count, vertical, columns)
    bands = lax.all_to_all(zonal, "slab", split_axis=2, concat_axis=0, tiled=True)
    item_count = bands.shape[1]
    band_width = bands.shape[2]
    merid = jnp.dot(
        merid_table,
        bands.reshape(total_rows, -1),
        preferred_element_type=jnp.float32,
        precision=PRECISE,
    )
    merid = merid.reshape(total_rows, item_count, band_width) * spectrum[:, None, :]
    back = jnp.dot(
        merid_table.T,
        merid.reshape(total_rows, -1),
        preferred_element_type=jnp.float32,
        precision=PRECISE,
    )
    back = back.reshape(total_rows, item_count, band_width)
    filtered = lax.all_to_all(back, "slab", split_axis=0, concat_axis=2, tiled=True)
    zonal_back = jnp.dot(
        filtered.reshape(-1, columns),
        zonal_table,
        preferred_element_type=jnp.float32,
        precision=PRECISE,
    )
    gradient = state_now + deviation * zonal_back.reshape(row_count, vertical, columns)
    return gradient[None]


HIGH = lax.Precision.HIGH
LANES = 128


def power_of_two(value):
    return value & (value - 1) == 0


def transposed_fits(chain_len, slabs, row_count, vertical, columns, observed):
    return (
        power_of_two(chain_len)
        and power_of_two(slabs)
        and vertical % chain_len == 0
        and vertical % slabs == 0
        and row_count % 8 == 0
        and columns % LANES == 0
        and row_count >= chain_len * STEPS
        and (chain_len * STEPS) % 8 == 0
        and observed % 8 == 0
    )


def exchange(value, axis, flip):
    count = lax.axis_size(axis)
    return lax.ppermute(value, axis, [(i, i ^ flip) for i in range(count)])


def dealt(blocks, axis):
    count = lax.axis_size(axis)
    me = lax.axis_index(axis)
    got = [lax.dynamic_index_in_dim(blocks, me, 0, keepdims=False)]
    for flip in range(1, count):
        got.append(exchange(lax.dynamic_index_in_dim(blocks, me ^ flip, 0, keepdims=False), axis, flip))
    return got


def neighbours(value, axis, dim, width):
    count = lax.axis_size(axis)
    size = value.shape[dim]
    tail = lax.slice_in_dim(value, size - width, size, axis=dim)
    head = lax.slice_in_dim(value, 0, width, axis=dim)
    before = lax.ppermute(tail, axis, [(i, i + 1) for i in range(count - 1)])
    after = lax.ppermute(head, axis, [(i + 1, i) for i in range(count - 1)])
    return before, after


def scatter_kernel(tile_ref, spot_ref, weight_ref, pull_ref, a_out, d_out, a_one, d_one, a_two, d_two):
    for ref in (a_one, d_one, a_two, d_two):
        ref[...] = jnp.zeros_like(ref)
    half = tile_ref.shape[0] // 2
    shape = a_one.shape[1:]
    place = lax.broadcasted_iota(jnp.int32, shape, 0) * LANES + lax.broadcasted_iota(jnp.int32, shape, 1)

    def add(entry, a_ref, d_ref):
        tile = tile_ref[entry]
        hit = place == spot_ref[entry]
        a_ref[tile] = a_ref[tile] + jnp.where(hit, weight_ref[entry], 0.0)
        d_ref[tile] = d_ref[tile] + jnp.where(hit, pull_ref[entry], 0.0)

    def four(group, carry):
        for inner in range(4):
            entry = group * 4 + inner
            add(entry, a_one, d_one)
            add(entry + half, a_two, d_two)
        return carry

    lax.fori_loop(0, half // 4, four, 0)
    across = a_out.shape[1] // LANES

    def store(group, carry):
        rows = pl.ds(pl.multiple_of(group * 8, 8), 8)
        for column in range(across):
            tile = group * across + column
            span = pl.ds(column * LANES, LANES)
            a_out[rows, span] = a_one[tile] + a_two[tile]
            d_out[rows, span] = d_one[tile] + d_two[tile]
        return carry

    lax.fori_loop(0, a_out.shape[0] // 8, store, 0)


def scatter(cells, weights, pulls, row_count, vertical, columns):
    row = cells // columns % vertical * row_count + cells // (vertical * columns)
    col = cells % columns
    tile = row // 8 * (columns // LANES) + col // LANES
    spot = row % 8 * LANES + col % LANES
    shape = (vertical * row_count, columns)
    tiles = (vertical * row_count // 8 * (columns // LANES), 8, LANES)
    smem = pl.BlockSpec(memory_space=pltpu.SMEM)
    return pl.pallas_call(
        scatter_kernel,
        out_shape=[jax.ShapeDtypeStruct(shape, jnp.float32)] * 2,
        in_specs=[smem] * 4,
        out_specs=[pl.BlockSpec(memory_space=pltpu.VMEM)] * 2,
        scratch_shapes=[pltpu.VMEM(tiles, jnp.float32)] * 4,
        cost_estimate=pl.CostEstimate(flops=0, bytes_accessed=160_000_000, transcendentals=0),
        name="observe",
    )(tile, spot, weights, pulls)


def load_coefficients(info, winds, above, below, slot, total_rows, coefs):
    centre, north, south, east, west = coefs
    halo = above.shape[2]
    height = centre.shape[0]
    columns = centre.shape[1]
    for low, piece in ((0, above), (halo, winds), (height - halo, below)):
        size = piece.shape[2]
        rows = lax.broadcasted_iota(jnp.int32, (size, columns), 0) + (info[1] + low)
        inside = jnp.where((rows >= 0) & (rows < total_rows), 1.0, 0.0)
        zonal = piece[slot, 0]
        merid = piece[slot, 1]
        span = pl.ds(low, size)
        centre[span] = (1.0 - 4.0 * DIFFUSION) * inside
        north[span] = (DIFFUSION - 0.5 * merid) * inside
        south[span] = (DIFFUSION + 0.5 * merid) * inside
        east[span] = (DIFFUSION - 0.5 * zonal) * inside
        west[span] = (DIFFUSION + 0.5 * zonal) * inside


def rolled(value, shift, axis):
    return pltpu.roll(value, shift % value.shape[axis], axis)


def tangent_kernel(total_rows, info, inc, inc_above, inc_below, winds, above, below, ends, state, *coefs):
    chain_len, fields, row_count, _ = inc.shape
    halo = inc_above.shape[2]
    height = state.shape[1]
    centre, north, south, east, west = coefs
    state[...] = jnp.zeros_like(state)

    def window(k, carry):
        slot = lax.bitwise_xor(k, info[0])
        load_coefficients(info, winds, above, below, slot, total_rows, coefs)
        state[:, 0:halo] = state[:, 0:halo] + inc_above[slot]
        state[:, halo : halo + row_count] = state[:, halo : halo + row_count] + inc[slot]
        state[:, halo + row_count : height] = state[:, halo + row_count : height] + inc_below[slot]

        def step(index, inner):
            for field in range(fields):
                now = state[field]
                state[field] = (
                    centre[...] * now
                    + north[...] * rolled(now, -1, 0)
                    + south[...] * rolled(now, 1, 0)
                    + east[...] * rolled(now, -1, 1)
                    + west[...] * rolled(now, 1, 1)
                )
            return inner

        lax.fori_loop(0, STEPS, step, 0)
        ends[slot] = state[:, halo : halo + row_count]
        return carry

    lax.fori_loop(0, chain_len, window, 0)


def adjoint_kernel(total_rows, info, seen, a_ref, d_ref, f_above, f_below, dev, winds, above, below, out, state, *coefs):
    chain_len, fields, row_count, _ = seen.shape
    halo = f_above.shape[2]
    height = state.shape[1]
    centre, north, south, east, west = coefs
    state[...] = jnp.zeros_like(state)

    def window(index, carry):
        k = chain_len - 1 - index
        slot = lax.bitwise_xor(k, info[0])
        load_coefficients(info, winds, above, below, slot, total_rows, coefs)
        state[:, 0:halo] = state[:, 0:halo] + f_above[slot]
        state[:, halo : halo + row_count] = state[:, halo : halo + row_count] + (
            a_ref[slot] * seen[slot] - d_ref[slot]
        )
        state[:, halo + row_count : height] = state[:, halo + row_count : height] + f_below[slot]

        def step(index, inner):
            for field in range(fields):
                now = state[field]
                state[field] = (
                    centre[...] * now
                    + rolled(north[...] * now, 1, 0)
                    + rolled(south[...] * now, -1, 0)
                    + rolled(east[...] * now, 1, 1)
                    + rolled(west[...] * now, -1, 1)
                )
            return inner

        lax.fori_loop(0, STEPS, step, 0)
        out[pl.ds(k * fields, fields)] = dev[...] * state[:, halo : halo + row_count]
        return carry

    lax.fori_loop(0, chain_len, window, 0)


def sweep(kernel, name, info, total_rows, out_shape, fields, height, columns, args):
    vmem = pl.BlockSpec(memory_space=pltpu.VMEM)
    return pl.pallas_call(
        functools.partial(kernel, total_rows),
        out_shape=jax.ShapeDtypeStruct(out_shape, jnp.float32),
        in_specs=[pl.BlockSpec(memory_space=pltpu.SMEM)] + [vmem] * len(args),
        out_specs=vmem,
        scratch_shapes=[pltpu.VMEM((fields, height, columns), jnp.float32)]
        + [pltpu.VMEM((height, columns), jnp.float32)] * 5,
        cost_estimate=pl.CostEstimate(flops=0, bytes_accessed=50_000_000, transcendentals=0),
        name=name,
    )(info, *args)


def transposed_body(increments, courant, deviation, spectrum, observed_cells, innovation, error_weights):
    own = increments[0]
    row_count, vertical, columns = own.shape
    chain_len = lax.axis_size("tm")
    slabs = lax.axis_size("slab")
    me = lax.axis_index("tm")
    slab = lax.axis_index("slab")
    total_rows = spectrum.shape[0]
    fields = vertical // chain_len
    halo = chain_len * STEPS
    height = row_count + 2 * halo
    block = (chain_len, fields, row_count, columns)
    info = jnp.stack([me, slab * row_count - halo]).astype(jnp.int32)

    incs = jnp.stack(dealt(own.transpose(1, 0, 2).reshape(block), "tm"))
    own_winds = courant[0].transpose(1, 0, 2)
    winds = jnp.stack([own_winds] + [exchange(own_winds, "tm", flip) for flip in range(1, chain_len)])
    bands = spectrum.T[None]
    flip = slabs // 2
    while flip:
        bands = jnp.concatenate([bands, exchange(bands, "slab", flip)])
        flip //= 2

    weights = error_weights[0]
    a_own, d_own = scatter(
        observed_cells[0], weights, weights * innovation[0], row_count, vertical, columns
    )
    a_all = jnp.stack(dealt(a_own.reshape(block), "tm"))
    d_all = jnp.stack(dealt(d_own.reshape(block), "tm"))

    inc_above, inc_below = neighbours(incs, "slab", 2, halo)
    above, below = neighbours(winds, "slab", 2, halo)
    ends = sweep(
        tangent_kernel, "tangent", info, total_rows, block, fields, height, columns,
        (incs, inc_above, inc_below, winds, above, below),
    )
    tail = row_count - halo
    f_above = a_all[:, :, tail:] * ends[:, :, tail:] - d_all[:, :, tail:]
    f_below = a_all[:, :, :halo] * ends[:, :, :halo] - d_all[:, :, :halo]
    f_above = lax.ppermute(f_above, "slab", [(i, i + 1) for i in range(slabs - 1)])
    f_below = lax.ppermute(f_below, "slab", [(i + 1, i) for i in range(slabs - 1)])
    dev = lax.dynamic_slice_in_dim(deviation, me * fields, fields, 1).transpose(1, 0, 2)
    scaled = sweep(
        adjoint_kernel, "adjoint", info, total_rows, (vertical, row_count, columns), fields, height, columns,
        (ends, a_all, d_all, f_above, f_below, dev, winds, above, below),
    )

    zonal_table = hartley_table(columns)
    merid_table = cosine_table(total_rows)
    share = vertical // slabs
    items = lax.all_to_all(
        scaled.reshape(slabs, share, row_count, columns), "slab", split_axis=0, concat_axis=0, tiled=True
    )
    items = items.transpose(1, 0, 2, 3).reshape(share, total_rows, columns)
    order = jnp.arange(slabs, dtype=jnp.int32) ^ slab
    place, bit, width = jnp.zeros_like(order), 1, slabs // 2
    while width:
        place = place + jnp.where((order & width) != 0, bit, 0)
        bit, width = bit * 2, width // 2
    variance = jnp.concatenate(
        [lax.dynamic_index_in_dim(bands, place[b], 0, keepdims=False) for b in range(slabs)]
    )
    done = []
    for item in range(share):
        zonal = jnp.dot(items[item], zonal_table, precision=HIGH, preferred_element_type=jnp.float32)
        merid = lax.dot_general(
            zonal, merid_table, (((0,), (1,)), ((), ())), precision=HIGH, preferred_element_type=jnp.float32
        )
        merid = merid * variance
        back = lax.dot_general(
            merid_table, merid, (((0,), (1,)), ((), ())), precision=HIGH, preferred_element_type=jnp.float32
        )
        done.append(jnp.dot(back, zonal_table, precision=HIGH, preferred_element_type=jnp.float32))
    filtered = jnp.stack(done).reshape(share, slabs, row_count, columns).transpose(1, 0, 2, 3)
    filtered = lax.all_to_all(filtered, "slab", split_axis=0, concat_axis=0, tiled=True)
    returned = dealt(filtered.reshape(block), "tm")
    home = jnp.zeros(block, jnp.float32)
    for flip in range(chain_len):
        home = lax.dynamic_update_index_in_dim(home, returned[flip], me ^ flip, 0)
    home = home.reshape(vertical, row_count, columns).transpose(1, 0, 2)
    return (own + deviation * home)[None]


def solution(mesh):
    in_specs = (
        P("tm", "slab", None, None),
        P("tm", "slab", None, None),
        P("slab", None, None),
        P(None, "slab"),
        P("tm", "slab"),
        P("tm", "slab"),
        P("tm", "slab"),
    )
    out_specs = P("tm", "slab", None, None)
    return jax.shard_map(body, mesh=mesh, in_specs=in_specs, out_specs=out_specs, check_vma=False)
```

```python
import functools
import math

import jax
import jax.numpy as jnp
from jax import lax
from jax.experimental import pallas as pl
from jax.experimental.pallas import tpu as pltpu
from jax.sharding import PartitionSpec as P

LEVELS = 2
STEPS = 4


DIFFUSION = 0.1
PRECISE = lax.Precision.HIGHEST


def with_halo(cells, sides, width):
    for axis, dim in sides:
        count = lax.axis_size(axis)
        ends = count - 1
        head = lax.slice_in_dim(cells, 0, width, axis=dim)
        tail = lax.slice_in_dim(cells, cells.shape[dim] - width, cells.shape[dim], axis=dim)
        cells = jnp.concatenate(
            [
                lax.ppermute(tail, axis, [(i, (i + 1) % count) for i in range(ends)]),
                cells,
                lax.ppermute(head, axis, [((i + 1) % count, i) for i in range(ends)]),
            ],
            axis=dim,
        )
    return cells


def from_behind(value, axis, steps):
    count = lax.axis_size(axis)
    first, last = (max(0, -steps), min(count, count - steps))
    return lax.ppermute(value, axis, [(source, source + steps) for source in range(first, last)])


def hartley_table(length):
    index = jnp.arange(length, dtype=jnp.int32)
    phase = index[:, None] * index[None, :] % length
    angle = phase.astype(jnp.float32) * (2.0 * math.pi / length)
    return (jnp.cos(angle) + jnp.sin(angle)) / math.sqrt(length)


def cosine_table(length):
    index = jnp.arange(length, dtype=jnp.int32)
    phase = (2 * index[None, :] + 1) * index[:, None] % (4 * length)
    angle = phase.astype(jnp.float32) * (math.pi / (2 * length))
    scales = jnp.where(index == 0, math.sqrt(1.0 / length), math.sqrt(2.0 / length)).astype(
        jnp.float32
    )
    return scales[:, None] * jnp.cos(angle)


def rims(values):
    return with_halo(values, (("slab", 0),), STEPS)


def forward_sweep(current, winds, inside):
    for step_index in range(STEPS):
        height = current.shape[0]
        lower = step_index + 1
        upper = lower + height - 2
        centre = current[1:-1]
        northern = current[2:]
        southern = current[:-2]
        eastern = jnp.roll(centre, -1, axis=2)
        western = jnp.roll(centre, 1, axis=2)
        local_winds = winds[lower:upper]
        zonal = local_winds[:, 0:1, :]
        meridional = local_winds[:, 1:2, :]
        spread = DIFFUSION * (northern + southern + eastern + western - 4.0 * centre)
        updated = (
            centre
            + spread
            - 0.5 * zonal * (eastern - western)
            - 0.5 * meridional * (northern - southern)
        )
        current = updated * inside[lower:upper]
    return current


def adjoint_sweep(current, winds, inside):
    for step_index in range(STEPS):
        height = current.shape[0]
        local_winds = winds[step_index : step_index + height]
        zonal_flux = local_winds[:, 0:1, :] * current
        merid_flux = local_winds[:, 1:2, :] * current
        centre = current[1:-1]
        northern = current[2:]
        southern = current[:-2]
        eastern = jnp.roll(centre, -1, axis=2)
        western = jnp.roll(centre, 1, axis=2)
        zonal_centre = zonal_flux[1:-1]
        spread = DIFFUSION * (northern + southern + eastern + western - 4.0 * centre)
        carried = 0.5 * (jnp.roll(zonal_centre, -1, axis=2) - jnp.roll(zonal_centre, 1, axis=2))
        carried = carried + 0.5 * (merid_flux[2:] - merid_flux[:-2])
        lower = step_index + 1
        current = (centre + spread + carried) * inside[lower : lower + height - 2]
    return current


def body(*arrays):
    row_count, vertical, columns = arrays[0].shape[1:]
    if transposed_fits(lax.axis_size("tm"), lax.axis_size("slab"), row_count, vertical, columns, arrays[4].shape[1]):
        return transposed_body(*arrays)
    return pipelined_body(*arrays)


def pipelined_body(increments, courant, deviation, spectrum, observed_cells, innovation, error_weights):
    state_now = increments[0]
    row_count, vertical, columns = state_now.shape
    chain_len = lax.axis_size("tm")
    position = lax.axis_index("tm")
    total_rows = spectrum.shape[0]
    first_row = lax.axis_index("slab") * row_count - STEPS
    global_rows = first_row + jnp.arange(row_count + 2 * STEPS, dtype=jnp.int32)
    inside = ((global_rows >= 0) & (global_rows < total_rows)).astype(jnp.float32)[:, None, None]
    winds = rims(courant[0])
    block_width = 2 * LEVELS
    block_count = vertical // block_width
    ticks = chain_len + block_count - 1
    empty_block = jnp.zeros((row_count, block_width, columns), jnp.float32)

    def forward_tick(tick, carry):
        arriving, ends = carry
        block = tick - position
        valid = (block >= 0) & (block < block_count)
        offset = jnp.clip(block, 0, block_count - 1) * block_width
        start = arriving + lax.dynamic_slice_in_dim(state_now, offset, block_width, 1)
        finish = forward_sweep(rims(start), winds, inside)
        ends = jnp.where(valid, lax.dynamic_update_slice_in_dim(ends, finish, offset, 1), ends)
        arriving = from_behind(finish, "tm", 1)
        return (arriving, ends)

    arrived, ends = lax.fori_loop(0, ticks, forward_tick, (empty_block, jnp.zeros_like(state_now)))
    cells = observed_cells[0]
    seen = ends.reshape(-1)[cells]
    misfit = error_weights[0] * (seen - innovation[0])
    forcing = jnp.zeros((row_count * vertical * columns,), jnp.float32).at[cells].add(misfit)
    forcing = forcing.reshape(row_count, vertical, columns)

    def backward_tick(tick, carry):
        arriving, starts = carry
        block = tick - (chain_len - 1 - position)
        valid = (block >= 0) & (block < block_count)
        offset = jnp.clip(block, 0, block_count - 1) * block_width
        ending = arriving + lax.dynamic_slice_in_dim(forcing, offset, block_width, 1)
        begun = adjoint_sweep(rims(ending), winds, inside)
        starts = jnp.where(valid, lax.dynamic_update_slice_in_dim(starts, begun, offset, 1), starts)
        arriving = from_behind(begun, "tm", -1)
        return (arriving, starts)

    returned, adjoint = lax.fori_loop(
        0, ticks, backward_tick, (empty_block, jnp.zeros_like(state_now))
    )
    zonal_table = hartley_table(columns)
    merid_table = cosine_table(total_rows)
    scaled = deviation * adjoint
    zonal = jnp.dot(
        scaled.reshape(-1, columns),
        zonal_table,
        preferred_element_type=jnp.float32,
        precision=PRECISE,
    )
    zonal = zonal.reshape(row_count, vertical, columns)
    bands = lax.all_to_all(zonal, "slab", split_axis=2, concat_axis=0, tiled=True)
    item_count = bands.shape[1]
    band_width = bands.shape[2]
    merid = jnp.dot(
        merid_table,
        bands.reshape(total_rows, -1),
        preferred_element_type=jnp.float32,
        precision=PRECISE,
    )
    merid = merid.reshape(total_rows, item_count, band_width) * spectrum[:, None, :]
    back = jnp.dot(
        merid_table.T,
        merid.reshape(total_rows, -1),
        preferred_element_type=jnp.float32,
        precision=PRECISE,
    )
    back = back.reshape(total_rows, item_count, band_width)
    filtered = lax.all_to_all(back, "slab", split_axis=0, concat_axis=2, tiled=True)
    zonal_back = jnp.dot(
        filtered.reshape(-1, columns),
        zonal_table,
        preferred_element_type=jnp.float32,
        precision=PRECISE,
    )
    gradient = state_now + deviation * zonal_back.reshape(row_count, vertical, columns)
    return gradient[None]


LANES = 128


def power_of_two(value):
    return value & (value - 1) == 0


def transposed_fits(chain_len, slabs, row_count, vertical, columns, observed):
    return (
        power_of_two(chain_len)
        and power_of_two(slabs)
        and vertical % chain_len == 0
        and vertical == slabs
        and row_count % 8 == 0
        and columns % LANES == 0
        and row_count >= chain_len * STEPS
        and (chain_len * STEPS) % 8 == 0
        and observed % 8 == 0
    )


def exchange(value, axis, flip):
    count = lax.axis_size(axis)
    return lax.ppermute(value, axis, [(i, i ^ flip) for i in range(count)])


def dealt(blocks, axis):
    count = lax.axis_size(axis)
    me = lax.axis_index(axis)
    got = [lax.dynamic_index_in_dim(blocks, me, 0, keepdims=False)]
    for flip in range(1, count):
        got.append(exchange(lax.dynamic_index_in_dim(blocks, me ^ flip, 0, keepdims=False), axis, flip))
    return got


def neighbours(value, axis, dim, width):
    count = lax.axis_size(axis)
    size = value.shape[dim]
    tail = lax.slice_in_dim(value, size - width, size, axis=dim)
    head = lax.slice_in_dim(value, 0, width, axis=dim)
    before = lax.ppermute(tail, axis, [(i, i + 1) for i in range(count - 1)])
    after = lax.ppermute(head, axis, [(i + 1, i) for i in range(count - 1)])
    return before, after


def scatter_kernel(tile_ref, spot_ref, weight_ref, pull_ref, a_out, d_out, a_one, d_one, a_two, d_two):
    for ref in (a_one, d_one, a_two, d_two):
        ref[...] = jnp.zeros_like(ref)
    half = tile_ref.shape[0] // 2
    shape = a_one.shape[1:]
    place = lax.broadcasted_iota(jnp.int32, shape, 0) * LANES + lax.broadcasted_iota(jnp.int32, shape, 1)

    def add(entry, a_ref, d_ref):
        tile = tile_ref[entry]
        hit = place == spot_ref[entry]
        a_ref[tile] = a_ref[tile] + jnp.where(hit, weight_ref[entry], 0.0)
        d_ref[tile] = d_ref[tile] + jnp.where(hit, pull_ref[entry], 0.0)

    def four(group, carry):
        for inner in range(4):
            entry = group * 4 + inner
            add(entry, a_one, d_one)
            add(entry + half, a_two, d_two)
        return carry

    lax.fori_loop(0, half // 4, four, 0)
    across = a_out.shape[1] // LANES

    def store(group, carry):
        rows = pl.ds(pl.multiple_of(group * 8, 8), 8)
        for column in range(across):
            tile = group * across + column
            span = pl.ds(column * LANES, LANES)
            a_out[rows, span] = a_one[tile] + a_two[tile]
            d_out[rows, span] = d_one[tile] + d_two[tile]
        return carry

    lax.fori_loop(0, a_out.shape[0] // 8, store, 0)


def scatter(cells, weights, pulls, row_count, vertical, columns):
    row = cells // columns % vertical * row_count + cells // (vertical * columns)
    col = cells % columns
    tile = row // 8 * (columns // LANES) + col // LANES
    spot = row % 8 * LANES + col % LANES
    shape = (vertical * row_count, columns)
    tiles = (vertical * row_count // 8 * (columns // LANES), 8, LANES)
    smem = pl.BlockSpec(memory_space=pltpu.SMEM)
    return pl.pallas_call(
        scatter_kernel,
        out_shape=[jax.ShapeDtypeStruct(shape, jnp.float32)] * 2,
        in_specs=[smem] * 4,
        out_specs=[pl.BlockSpec(memory_space=pltpu.VMEM)] * 2,
        scratch_shapes=[pltpu.VMEM(tiles, jnp.float32)] * 4,
        cost_estimate=pl.CostEstimate(flops=0, bytes_accessed=160_000_000, transcendentals=0),
        name="observe",
    )(tile, spot, weights, pulls)


def load_coefficients(info, winds, above, below, slot, total_rows, coefs):
    centre, north, south, east, west = coefs
    halo = above.shape[2]
    height = centre.shape[0]
    columns = centre.shape[1]
    for low, piece in ((0, above), (halo, winds), (height - halo, below)):
        size = piece.shape[2]
        rows = lax.broadcasted_iota(jnp.int32, (size, columns), 0) + (info[1] + low)
        inside = jnp.where((rows >= 0) & (rows < total_rows), 1.0, 0.0)
        zonal = piece[slot, 0]
        merid = piece[slot, 1]
        span = pl.ds(low, size)
        centre[span] = (1.0 - 4.0 * DIFFUSION) * inside
        north[span] = (DIFFUSION - 0.5 * merid) * inside
        south[span] = (DIFFUSION + 0.5 * merid) * inside
        east[span] = (DIFFUSION - 0.5 * zonal) * inside
        west[span] = (DIFFUSION + 0.5 * zonal) * inside


def rolled(value, shift, axis):
    return pltpu.roll(value, shift % value.shape[axis], axis)


def tangent_kernel(total_rows, info, inc, inc_above, inc_below, winds, above, below, _variance, ends, state, *coefs):
    chain_len, fields, row_count, _ = inc.shape
    halo = inc_above.shape[2]
    height = state.shape[1]
    centre, north, south, east, west = coefs
    state[...] = jnp.zeros_like(state)

    def window(k, carry):
        slot = lax.bitwise_xor(k, info[0])
        load_coefficients(info, winds, above, below, slot, total_rows, coefs)
        state[:, 0:halo] = state[:, 0:halo] + inc_above[slot]
        state[:, halo : halo + row_count] = state[:, halo : halo + row_count] + inc[slot]
        state[:, halo + row_count : height] = state[:, halo + row_count : height] + inc_below[slot]

        def step(index, inner):
            for field in range(fields):
                now = state[field]
                state[field] = (
                    centre[...] * now
                    + north[...] * rolled(now, -1, 0)
                    + south[...] * rolled(now, 1, 0)
                    + east[...] * rolled(now, -1, 1)
                    + west[...] * rolled(now, 1, 1)
                )
            return inner

        lax.fori_loop(0, STEPS, step, 0)
        ends[slot] = state[:, halo : halo + row_count]
        return carry

    lax.fori_loop(0, chain_len, window, 0)


def adjoint_kernel(total_rows, info, seen, f_above, f_below, dev, winds, above, below, *rest):
    chain_len, fields, row_count, _ = seen.shape
    a_refs, d_refs = rest[:chain_len], rest[chain_len : 2 * chain_len]
    out, state, *coefs = rest[2 * chain_len :]
    halo = f_above.shape[2]
    height = state.shape[1]
    centre, north, south, east, west = coefs
    state[...] = jnp.zeros_like(state)

    def window(index, carry):
        k = chain_len - 1 - index
        slot = lax.bitwise_xor(k, info[0])
        load_coefficients(info, winds, above, below, slot, total_rows, coefs)
        state[:, 0:halo] = state[:, 0:halo] + f_above[slot]
        for flip in range(chain_len):

            @pl.when(slot == flip)
            def _():
                state[:, halo : halo + row_count] = state[:, halo : halo + row_count] + (
                    a_refs[flip][...] * seen[flip] - d_refs[flip][...]
                )

        state[:, halo + row_count : height] = state[:, halo + row_count : height] + f_below[slot]

        def step(index, inner):
            for field in range(fields):
                now = state[field]
                state[field] = (
                    centre[...] * now
                    + rolled(north[...] * now, 1, 0)
                    + rolled(south[...] * now, -1, 0)
                    + rolled(east[...] * now, 1, 1)
                    + rolled(west[...] * now, -1, 1)
                )
            return inner

        lax.fori_loop(0, STEPS, step, 0)
        out[pl.ds(k * fields, fields)] = dev[...] * state[:, halo : halo + row_count]
        return carry

    lax.fori_loop(0, chain_len, window, 0)


def sweep(kernel, name, info, total_rows, out_shape, fields, height, columns, args, ready=()):
    vmem = pl.BlockSpec(memory_space=pltpu.VMEM)
    return pl.pallas_call(
        functools.partial(kernel, total_rows),
        out_shape=jax.ShapeDtypeStruct(out_shape, jnp.float32),
        in_specs=[pl.BlockSpec(memory_space=pltpu.SMEM)] + [vmem] * len(args)
        + [pl.BlockSpec(memory_space=pl.ANY)] * len(ready),
        out_specs=vmem,
        scratch_shapes=[pltpu.VMEM((fields, height, columns), jnp.float32)]
        + [pltpu.VMEM((height, columns), jnp.float32)] * 5,
        cost_estimate=pl.CostEstimate(flops=0, bytes_accessed=50_000_000, transcendentals=0),
        name=name,
    )(info, *args, *ready)


def halves(value):
    top = value.astype(jnp.bfloat16)
    return top, (value - top.astype(jnp.float32)).astype(jnp.bfloat16)


def product(left, right):
    dot = functools.partial(jnp.dot, preferred_element_type=jnp.float32)
    return dot(left[0], right[0]) + (dot(left[0], right[1]) + dot(left[1], right[0]))


def covariance_kernel(item, h_top, h_low, c_top, c_low, t_top, t_low, variance, out, a_top, a_low, b_top, b_low):
    total = item.shape[0]
    tile = next(size for size in (256, 128, 64, 32, 16, 8) if total % size == 0)

    def tiles(work):
        def one(index, carry):
            work(pl.ds(pl.multiple_of(index * tile, tile), tile))
            return carry

        lax.fori_loop(0, total // tile, one, 0)

    def zonal(rows):
        a_top[rows], a_low[rows] = halves(product(halves(item[rows]), (h_top[...], h_low[...])))

    def merid(rows):
        spectral = product((c_top[rows], c_low[rows]), (a_top[...], a_low[...]))
        b_top[rows], b_low[rows] = halves(spectral * variance[rows])

    def merid_back(rows):
        a_top[rows], a_low[rows] = halves(product((t_top[rows], t_low[rows]), (b_top[...], b_low[...])))

    def zonal_back(rows):
        out[rows] = product((a_top[rows], a_low[rows]), (h_top[...], h_low[...]))

    tiles(zonal)
    tiles(merid)
    tiles(merid_back)
    tiles(zonal_back)


def table_halves(table):
    top = lax.reduce_precision(table, 8, 7)
    return top.astype(jnp.bfloat16), (table - top).astype(jnp.bfloat16)


def covariance(item, variance):
    total, columns = item.shape
    merid_table = cosine_table(total)
    vmem = pl.BlockSpec(memory_space=pltpu.VMEM)
    half = pltpu.VMEM((total, columns), jnp.bfloat16)
    return pl.pallas_call(
        covariance_kernel,
        out_shape=jax.ShapeDtypeStruct((total, columns), jnp.float32),
        in_specs=[vmem] * 8,
        out_specs=vmem,
        scratch_shapes=[half] * 4,
        cost_estimate=pl.CostEstimate(
            flops=24 * total * total * columns, bytes_accessed=60_000_000, transcendentals=0
        ),
        name="covariance",
    )(
        item,
        *table_halves(hartley_table(columns)),
        *table_halves(merid_table),
        *table_halves(merid_table.T),
        variance,
    )


def sent_home(chunks, chain_len, slabs, fields):
    field = lax.axis_index("tm") * fields + lax.axis_index("slab") % fields
    received = []
    for flip in range(slabs):
        pairs = [
            (j * slabs + s, s // fields * slabs + ((j * fields + s % fields) ^ flip))
            for j in range(chain_len)
            for s in range(slabs)
        ]
        chunk = lax.dynamic_index_in_dim(chunks, field ^ flip, 0, keepdims=False)
        received.append(lax.ppermute(chunk, ("tm", "slab"), pairs))
    return received


def transposed_body(increments, courant, deviation, spectrum, observed_cells, innovation, error_weights):
    own = increments[0]
    row_count, vertical, columns = own.shape
    chain_len = lax.axis_size("tm")
    slabs = lax.axis_size("slab")
    me = lax.axis_index("tm")
    slab = lax.axis_index("slab")
    total_rows = spectrum.shape[0]
    fields = vertical // chain_len
    halo = chain_len * STEPS
    height = row_count + 2 * halo
    block = (chain_len, fields, row_count, columns)
    info = jnp.stack([me, slab * row_count - halo]).astype(jnp.int32)

    incs = jnp.stack(dealt(own.transpose(1, 0, 2).reshape(block), "tm"))
    own_winds = courant[0].transpose(1, 0, 2)
    winds = jnp.stack([own_winds] + [exchange(own_winds, "tm", flip) for flip in range(1, chain_len)])
    bands = spectrum.T[None]
    flip = slabs // 2
    while flip:
        bands = jnp.concatenate([bands, exchange(bands, "slab", flip)])
        flip //= 2

    order = jnp.arange(slabs, dtype=jnp.int32) ^ slab
    place, bit, width = jnp.zeros_like(order), 1, slabs // 2
    while width:
        place = place + jnp.where((order & width) != 0, bit, 0)
        bit, width = bit * 2, width // 2
    variance = jnp.concatenate(
        [lax.dynamic_index_in_dim(bands, place[b], 0, keepdims=False) for b in range(slabs)]
    ).T
    weights = error_weights[0]
    a_own, d_own = scatter(
        observed_cells[0], weights, weights * innovation[0], row_count, vertical, columns
    )
    a_got = dealt(a_own.reshape(block), "tm")
    d_got = dealt(d_own.reshape(block), "tm")

    inc_above, inc_below = neighbours(incs, "slab", 2, halo)
    above, below = neighbours(winds, "slab", 2, halo)
    ends = sweep(
        tangent_kernel, "tangent", info, total_rows, block, fields, height, columns,
        (incs, inc_above, inc_below, winds, above, below), (variance,),
    )
    tail = row_count - halo
    f_above = jnp.stack([a[:, tail:] * x[:, tail:] - d[:, tail:] for a, x, d in zip(a_got, ends, d_got)])
    f_below = jnp.stack([a[:, :halo] * x[:, :halo] - d[:, :halo] for a, x, d in zip(a_got, ends, d_got)])
    f_above = lax.ppermute(f_above, "slab", [(i, i + 1) for i in range(slabs - 1)])
    f_below = lax.ppermute(f_below, "slab", [(i + 1, i) for i in range(slabs - 1)])
    dev = lax.dynamic_slice_in_dim(deviation, me * fields, fields, 1).transpose(1, 0, 2)
    scaled = sweep(
        adjoint_kernel, "adjoint", info, total_rows, (vertical, row_count, columns), fields, height, columns,
        (ends, f_above, f_below, dev, winds, above, below, *a_got, *d_got),
    )

    items = lax.all_to_all(scaled, "slab", split_axis=0, concat_axis=0, tiled=True)
    filtered = covariance(items.reshape(total_rows, columns), variance)
    received = jnp.stack(sent_home(filtered.reshape(slabs, row_count, columns), chain_len, slabs, fields))
    home = jnp.stack(
        [lax.dynamic_index_in_dim(received, slab ^ field, 0, keepdims=False) for field in range(vertical)]
    )
    return (own + deviation * home.transpose(1, 0, 2))[None]


def solution(mesh):
    in_specs = (
        P("tm", "slab", None, None),
        P("tm", "slab", None, None),
        P("slab", None, None),
        P(None, "slab"),
        P("tm", "slab"),
        P("tm", "slab"),
        P("tm", "slab"),
    )
    out_specs = P("tm", "slab", None, None)
    return jax.shard_map(body, mesh=mesh, in_specs=in_specs, out_specs=out_specs, check_vma=False)
```

```python
import functools
import math

import jax
import jax.numpy as jnp
from jax import lax
from jax.experimental import pallas as pl
from jax.experimental.pallas import tpu as pltpu
from jax.sharding import PartitionSpec as P

LEVELS = 2
STEPS = 4


DIFFUSION = 0.1
PRECISE = lax.Precision.HIGHEST


def with_halo(cells, sides, width):
    for axis, dim in sides:
        count = lax.axis_size(axis)
        ends = count - 1
        head = lax.slice_in_dim(cells, 0, width, axis=dim)
        tail = lax.slice_in_dim(cells, cells.shape[dim] - width, cells.shape[dim], axis=dim)
        cells = jnp.concatenate(
            [
                lax.ppermute(tail, axis, [(i, (i + 1) % count) for i in range(ends)]),
                cells,
                lax.ppermute(head, axis, [((i + 1) % count, i) for i in range(ends)]),
            ],
            axis=dim,
        )
    return cells


def from_behind(value, axis, steps):
    count = lax.axis_size(axis)
    first, last = (max(0, -steps), min(count, count - steps))
    return lax.ppermute(value, axis, [(source, source + steps) for source in range(first, last)])


def hartley_table(length):
    index = jnp.arange(length, dtype=jnp.int32)
    phase = index[:, None] * index[None, :] % length
    angle = phase.astype(jnp.float32) * (2.0 * math.pi / length)
    return (jnp.cos(angle) + jnp.sin(angle)) / math.sqrt(length)


def cosine_table(length):
    index = jnp.arange(length, dtype=jnp.int32)
    phase = (2 * index[None, :] + 1) * index[:, None] % (4 * length)
    angle = phase.astype(jnp.float32) * (math.pi / (2 * length))
    scales = jnp.where(index == 0, math.sqrt(1.0 / length), math.sqrt(2.0 / length)).astype(
        jnp.float32
    )
    return scales[:, None] * jnp.cos(angle)


def rims(values):
    return with_halo(values, (("slab", 0),), STEPS)


def forward_sweep(current, winds, inside):
    for step_index in range(STEPS):
        height = current.shape[0]
        lower = step_index + 1
        upper = lower + height - 2
        centre = current[1:-1]
        northern = current[2:]
        southern = current[:-2]
        eastern = jnp.roll(centre, -1, axis=2)
        western = jnp.roll(centre, 1, axis=2)
        local_winds = winds[lower:upper]
        zonal = local_winds[:, 0:1, :]
        meridional = local_winds[:, 1:2, :]
        spread = DIFFUSION * (northern + southern + eastern + western - 4.0 * centre)
        updated = (
            centre
            + spread
            - 0.5 * zonal * (eastern - western)
            - 0.5 * meridional * (northern - southern)
        )
        current = updated * inside[lower:upper]
    return current


def adjoint_sweep(current, winds, inside):
    for step_index in range(STEPS):
        height = current.shape[0]
        local_winds = winds[step_index : step_index + height]
        zonal_flux = local_winds[:, 0:1, :] * current
        merid_flux = local_winds[:, 1:2, :] * current
        centre = current[1:-1]
        northern = current[2:]
        southern = current[:-2]
        eastern = jnp.roll(centre, -1, axis=2)
        western = jnp.roll(centre, 1, axis=2)
        zonal_centre = zonal_flux[1:-1]
        spread = DIFFUSION * (northern + southern + eastern + western - 4.0 * centre)
        carried = 0.5 * (jnp.roll(zonal_centre, -1, axis=2) - jnp.roll(zonal_centre, 1, axis=2))
        carried = carried + 0.5 * (merid_flux[2:] - merid_flux[:-2])
        lower = step_index + 1
        current = (centre + spread + carried) * inside[lower : lower + height - 2]
    return current


def body(*arrays):
    row_count, vertical, columns = arrays[0].shape[1:]
    if transposed_fits(lax.axis_size("tm"), lax.axis_size("slab"), row_count, vertical, columns, arrays[4].shape[1]):
        return transposed_body(*arrays)
    return pipelined_body(*arrays)


def pipelined_body(increments, courant, deviation, spectrum, observed_cells, innovation, error_weights):
    state_now = increments[0]
    row_count, vertical, columns = state_now.shape
    chain_len = lax.axis_size("tm")
    position = lax.axis_index("tm")
    total_rows = spectrum.shape[0]
    first_row = lax.axis_index("slab") * row_count - STEPS
    global_rows = first_row + jnp.arange(row_count + 2 * STEPS, dtype=jnp.int32)
    inside = ((global_rows >= 0) & (global_rows < total_rows)).astype(jnp.float32)[:, None, None]
    winds = rims(courant[0])
    block_width = 2 * LEVELS
    block_count = vertical // block_width
    ticks = chain_len + block_count - 1
    empty_block = jnp.zeros((row_count, block_width, columns), jnp.float32)

    def forward_tick(tick, carry):
        arriving, ends = carry
        block = tick - position
        valid = (block >= 0) & (block < block_count)
        offset = jnp.clip(block, 0, block_count - 1) * block_width
        start = arriving + lax.dynamic_slice_in_dim(state_now, offset, block_width, 1)
        finish = forward_sweep(rims(start), winds, inside)
        ends = jnp.where(valid, lax.dynamic_update_slice_in_dim(ends, finish, offset, 1), ends)
        arriving = from_behind(finish, "tm", 1)
        return (arriving, ends)

    arrived, ends = lax.fori_loop(0, ticks, forward_tick, (empty_block, jnp.zeros_like(state_now)))
    cells = observed_cells[0]
    seen = ends.reshape(-1)[cells]
    misfit = error_weights[0] * (seen - innovation[0])
    forcing = jnp.zeros((row_count * vertical * columns,), jnp.float32).at[cells].add(misfit)
    forcing = forcing.reshape(row_count, vertical, columns)

    def backward_tick(tick, carry):
        arriving, starts = carry
        block = tick - (chain_len - 1 - position)
        valid = (block >= 0) & (block < block_count)
        offset = jnp.clip(block, 0, block_count - 1) * block_width
        ending = arriving + lax.dynamic_slice_in_dim(forcing, offset, block_width, 1)
        begun = adjoint_sweep(rims(ending), winds, inside)
        starts = jnp.where(valid, lax.dynamic_update_slice_in_dim(starts, begun, offset, 1), starts)
        arriving = from_behind(begun, "tm", -1)
        return (arriving, starts)

    returned, adjoint = lax.fori_loop(
        0, ticks, backward_tick, (empty_block, jnp.zeros_like(state_now))
    )
    zonal_table = hartley_table(columns)
    merid_table = cosine_table(total_rows)
    scaled = deviation * adjoint
    zonal = jnp.dot(
        scaled.reshape(-1, columns),
        zonal_table,
        preferred_element_type=jnp.float32,
        precision=PRECISE,
    )
    zonal = zonal.reshape(row_count, vertical, columns)
    bands = lax.all_to_all(zonal, "slab", split_axis=2, concat_axis=0, tiled=True)
    item_count = bands.shape[1]
    band_width = bands.shape[2]
    merid = jnp.dot(
        merid_table,
        bands.reshape(total_rows, -1),
        preferred_element_type=jnp.float32,
        precision=PRECISE,
    )
    merid = merid.reshape(total_rows, item_count, band_width) * spectrum[:, None, :]
    back = jnp.dot(
        merid_table.T,
        merid.reshape(total_rows, -1),
        preferred_element_type=jnp.float32,
        precision=PRECISE,
    )
    back = back.reshape(total_rows, item_count, band_width)
    filtered = lax.all_to_all(back, "slab", split_axis=0, concat_axis=2, tiled=True)
    zonal_back = jnp.dot(
        filtered.reshape(-1, columns),
        zonal_table,
        preferred_element_type=jnp.float32,
        precision=PRECISE,
    )
    gradient = state_now + deviation * zonal_back.reshape(row_count, vertical, columns)
    return gradient[None]


LANES = 128


def power_of_two(value):
    return value & (value - 1) == 0


def transposed_fits(chain_len, slabs, row_count, vertical, columns, observed):
    return (
        power_of_two(chain_len)
        and power_of_two(slabs)
        and vertical % chain_len == 0
        and vertical == slabs
        and row_count % 8 == 0
        and columns % LANES == 0
        and row_count >= chain_len * STEPS
        and (chain_len * STEPS) % 8 == 0
        and observed % 8 == 0
    )


def exchange(value, axis, flip):
    count = lax.axis_size(axis)
    return lax.ppermute(value, axis, [(i, i ^ flip) for i in range(count)])


def dealt(blocks, axis):
    count = lax.axis_size(axis)
    me = lax.axis_index(axis)
    got = [lax.dynamic_index_in_dim(blocks, me, 0, keepdims=False)]
    for flip in range(1, count):
        got.append(exchange(lax.dynamic_index_in_dim(blocks, me ^ flip, 0, keepdims=False), axis, flip))
    return got


def neighbours(value, axis, dim, width):
    count = lax.axis_size(axis)
    size = value.shape[dim]
    tail = lax.slice_in_dim(value, size - width, size, axis=dim)
    head = lax.slice_in_dim(value, 0, width, axis=dim)
    before = lax.ppermute(tail, axis, [(i, i + 1) for i in range(count - 1)])
    after = lax.ppermute(head, axis, [(i + 1, i) for i in range(count - 1)])
    return before, after


def scatter_kernel(tile_ref, spot_ref, weight_ref, pull_ref, a_out, d_out, a_one, d_one, a_two, d_two):
    for ref in (a_one, d_one, a_two, d_two):
        ref[...] = jnp.zeros_like(ref)
    half = tile_ref.shape[0] // 2
    shape = a_one.shape[1:]
    place = lax.broadcasted_iota(jnp.int32, shape, 0) * LANES + lax.broadcasted_iota(jnp.int32, shape, 1)

    def add(entry, a_ref, d_ref):
        tile = tile_ref[entry]
        hit = place == spot_ref[entry]
        a_ref[tile] = a_ref[tile] + jnp.where(hit, weight_ref[entry], 0.0)
        d_ref[tile] = d_ref[tile] + jnp.where(hit, pull_ref[entry], 0.0)

    def four(group, carry):
        for inner in range(4):
            entry = group * 4 + inner
            add(entry, a_one, d_one)
            add(entry + half, a_two, d_two)
        return carry

    lax.fori_loop(0, half // 4, four, 0)
    across = a_out.shape[1] // LANES

    def store(group, carry):
        rows = pl.ds(pl.multiple_of(group * 8, 8), 8)
        for column in range(across):
            tile = group * across + column
            span = pl.ds(column * LANES, LANES)
            a_out[rows, span] = a_one[tile] + a_two[tile]
            d_out[rows, span] = d_one[tile] + d_two[tile]
        return carry

    lax.fori_loop(0, a_out.shape[0] // 8, store, 0)


def scatter(cells, weights, pulls, row_count, vertical, columns):
    row = cells // columns % vertical * row_count + cells // (vertical * columns)
    col = cells % columns
    tile = row // 8 * (columns // LANES) + col // LANES
    spot = row % 8 * LANES + col % LANES
    shape = (vertical * row_count, columns)
    tiles = (vertical * row_count // 8 * (columns // LANES), 8, LANES)
    smem = pl.BlockSpec(memory_space=pltpu.SMEM)
    return pl.pallas_call(
        scatter_kernel,
        out_shape=[jax.ShapeDtypeStruct(shape, jnp.float32)] * 2,
        in_specs=[smem] * 4,
        out_specs=[pl.BlockSpec(memory_space=pltpu.VMEM)] * 2,
        scratch_shapes=[pltpu.VMEM(tiles, jnp.float32)] * 4,
        cost_estimate=pl.CostEstimate(flops=0, bytes_accessed=160_000_000, transcendentals=0),
        name="observe",
    )(tile, spot, weights, pulls)


def load_coefficients(info, winds, above, below, slot, total_rows, coefs):
    centre, north, south, east, west = coefs
    halo = above.shape[2]
    height = centre.shape[0]
    columns = centre.shape[1]
    for low, piece in ((0, above), (halo, winds), (height - halo, below)):
        size = piece.shape[2]
        rows = lax.broadcasted_iota(jnp.int32, (size, columns), 0) + (info[1] + low)
        inside = jnp.where((rows >= 0) & (rows < total_rows), 1.0, 0.0)
        zonal = piece[slot, 0]
        merid = piece[slot, 1]
        span = pl.ds(low, size)
        centre[span] = (1.0 - 4.0 * DIFFUSION) * inside
        north[span] = (DIFFUSION - 0.5 * merid) * inside
        south[span] = (DIFFUSION + 0.5 * merid) * inside
        east[span] = (DIFFUSION - 0.5 * zonal) * inside
        west[span] = (DIFFUSION + 0.5 * zonal) * inside


def rolled(value, shift, axis):
    return pltpu.roll(value, shift % value.shape[axis], axis)


def tangent_kernel(total_rows, info, inc, inc_above, inc_below, winds, above, below, _gathered, ends, state, *coefs):
    chain_len, fields, row_count, _ = inc.shape
    halo = inc_above.shape[2]
    height = state.shape[1]
    centre, north, south, east, west = coefs
    state[...] = jnp.zeros_like(state)

    def window(k, carry):
        slot = lax.bitwise_xor(k, info[0])
        load_coefficients(info, winds, above, below, slot, total_rows, coefs)
        state[:, 0:halo] = state[:, 0:halo] + inc_above[slot]
        state[:, halo : halo + row_count] = state[:, halo : halo + row_count] + inc[slot]
        state[:, halo + row_count : height] = state[:, halo + row_count : height] + inc_below[slot]

        def step(index, inner):
            for field in range(fields):
                now = state[field]
                state[field] = (
                    centre[...] * now
                    + north[...] * rolled(now, -1, 0)
                    + south[...] * rolled(now, 1, 0)
                    + east[...] * rolled(now, -1, 1)
                    + west[...] * rolled(now, 1, 1)
                )
            return inner

        lax.fori_loop(0, STEPS, step, 0)
        ends[slot] = state[:, halo : halo + row_count]
        return carry

    lax.fori_loop(0, chain_len, window, 0)


def adjoint_kernel(total_rows, info, seen, f_above, f_below, dev, winds, above, below, *rest):
    chain_len, fields, row_count, _ = seen.shape
    a_refs, d_refs = rest[:chain_len], rest[chain_len : 2 * chain_len]
    out, state, *coefs = rest[2 * chain_len :]
    halo = f_above.shape[2]
    height = state.shape[1]
    centre, north, south, east, west = coefs
    state[...] = jnp.zeros_like(state)

    def window(index, carry):
        k = chain_len - 1 - index
        slot = lax.bitwise_xor(k, info[0])
        load_coefficients(info, winds, above, below, slot, total_rows, coefs)
        state[:, 0:halo] = state[:, 0:halo] + f_above[slot]
        for flip in range(chain_len):

            @pl.when(slot == flip)
            def _():
                state[:, halo : halo + row_count] = state[:, halo : halo + row_count] + (
                    a_refs[flip][...] * seen[flip] - d_refs[flip][...]
                )

        state[:, halo + row_count : height] = state[:, halo + row_count : height] + f_below[slot]

        def step(index, inner):
            for field in range(fields):
                now = state[field]
                state[field] = (
                    centre[...] * now
                    + rolled(north[...] * now, 1, 0)
                    + rolled(south[...] * now, -1, 0)
                    + rolled(east[...] * now, 1, 1)
                    + rolled(west[...] * now, -1, 1)
                )
            return inner

        lax.fori_loop(0, STEPS, step, 0)
        out[pl.ds(k * fields, fields)] = dev[...] * state[:, halo : halo + row_count]
        return carry

    lax.fori_loop(0, chain_len, window, 0)


def sweep(kernel, name, info, total_rows, out_shape, fields, height, columns, args, ready=()):
    vmem = pl.BlockSpec(memory_space=pltpu.VMEM)
    return pl.pallas_call(
        functools.partial(kernel, total_rows),
        out_shape=jax.ShapeDtypeStruct(out_shape, jnp.float32),
        in_specs=[pl.BlockSpec(memory_space=pltpu.SMEM)] + [vmem] * len(args)
        + [pl.BlockSpec(memory_space=pl.ANY)] * len(ready),
        out_specs=vmem,
        scratch_shapes=[pltpu.VMEM((fields, height, columns), jnp.float32)]
        + [pltpu.VMEM((height, columns), jnp.float32)] * 5,
        cost_estimate=pl.CostEstimate(flops=0, bytes_accessed=50_000_000, transcendentals=0),
        name=name,
    )(info, *args, *ready)


def halves(value):
    top = value.astype(jnp.bfloat16)
    return top, (value - top.astype(jnp.float32)).astype(jnp.bfloat16)


def product(left, right):
    dot = functools.partial(jnp.dot, preferred_element_type=jnp.float32)
    return dot(left[0], right[0]) + (dot(left[0], right[1]) + dot(left[1], right[0]))


def covariance_kernel(item, h_top, h_low, c_top, c_low, t_top, t_low, variance, out, a_top, a_low, b_top, b_low):
    total = item.shape[0]
    tile = next(size for size in (256, 128, 64, 32, 16, 8) if total % size == 0)

    def tiles(work):
        def one(index, carry):
            work(pl.ds(pl.multiple_of(index * tile, tile), tile))
            return carry

        lax.fori_loop(0, total // tile, one, 0)

    def zonal(rows):
        a_top[rows], a_low[rows] = halves(product(halves(item[rows]), (h_top[...], h_low[...])))

    def merid(rows):
        spectral = product((c_top[rows], c_low[rows]), (a_top[...], a_low[...]))
        b_top[rows], b_low[rows] = halves(spectral * variance[rows])

    def merid_back(rows):
        a_top[rows], a_low[rows] = halves(product((t_top[rows], t_low[rows]), (b_top[...], b_low[...])))

    def zonal_back(rows):
        out[rows] = product((a_top[rows], a_low[rows]), (h_top[...], h_low[...]))

    tiles(zonal)
    tiles(merid)
    tiles(merid_back)
    tiles(zonal_back)


def table_halves(table):
    top = lax.reduce_precision(table, 8, 7)
    return top.astype(jnp.bfloat16), (table - top).astype(jnp.bfloat16)


def covariance(item, variance):
    total, columns = item.shape
    merid_table = cosine_table(total)
    vmem = pl.BlockSpec(memory_space=pltpu.VMEM)
    half = pltpu.VMEM((total, columns), jnp.bfloat16)
    return pl.pallas_call(
        covariance_kernel,
        out_shape=jax.ShapeDtypeStruct((total, columns), jnp.float32),
        in_specs=[vmem] * 8,
        out_specs=vmem,
        scratch_shapes=[half] * 4,
        cost_estimate=pl.CostEstimate(
            flops=24 * total * total * columns, bytes_accessed=60_000_000, transcendentals=0
        ),
        name="covariance",
    )(
        item,
        *table_halves(hartley_table(columns)),
        *table_halves(merid_table),
        *table_halves(merid_table.T),
        variance,
    )


def sent_home(chunks, chain_len, slabs, fields):
    field = lax.axis_index("tm") * fields + lax.axis_index("slab") % fields
    received = []
    for flip in range(slabs):
        pairs = [
            (j * slabs + s, s // fields * slabs + ((j * fields + s % fields) ^ flip))
            for j in range(chain_len)
            for s in range(slabs)
        ]
        chunk = lax.dynamic_index_in_dim(chunks, field ^ flip, 0, keepdims=False)
        received.append(lax.ppermute(chunk, ("tm", "slab"), pairs))
    return received


def gradient_kernel(slab, own, deviation, *rest):
    received, (out, home) = rest[:-2], rest[-2:]
    for flip, block in enumerate(received):
        home[lax.bitwise_xor(slab[0], flip)] = block[...]

    def eight(group, carry):
        rows = pl.ds(pl.multiple_of(group * 8, 8), 8)
        filtered = jnp.swapaxes(home[:, rows, :], 0, 1)
        out[rows] = own[rows] + deviation[rows] * filtered
        return carry

    lax.fori_loop(0, own.shape[0] // 8, eight, 0)


def transposed_body(increments, courant, deviation, spectrum, observed_cells, innovation, error_weights):
    own = increments[0]
    row_count, vertical, columns = own.shape
    chain_len = lax.axis_size("tm")
    slabs = lax.axis_size("slab")
    me = lax.axis_index("tm")
    slab = lax.axis_index("slab")
    total_rows = spectrum.shape[0]
    fields = vertical // chain_len
    halo = chain_len * STEPS
    height = row_count + 2 * halo
    block = (chain_len, fields, row_count, columns)
    info = jnp.stack([me, slab * row_count - halo]).astype(jnp.int32)

    incs = jnp.stack(dealt(own.transpose(1, 0, 2).reshape(block), "tm"))
    own_winds = courant[0].transpose(1, 0, 2)
    winds = jnp.stack([own_winds] + [exchange(own_winds, "tm", flip) for flip in range(1, chain_len)])
    bands = spectrum.T[None]
    flip = slabs // 2
    while flip:
        gathered = exchange(bands, "slab", flip)
        bands = jnp.concatenate([bands, gathered])
        flip //= 2

    weights = error_weights[0]
    a_own, d_own = scatter(
        observed_cells[0], weights, weights * innovation[0], row_count, vertical, columns
    )
    a_got = dealt(a_own.reshape(block), "tm")
    d_got = dealt(d_own.reshape(block), "tm")

    inc_above, inc_below = neighbours(incs, "slab", 2, halo)
    above, below = neighbours(winds, "slab", 2, halo)
    ends = sweep(
        tangent_kernel, "tangent", info, total_rows, block, fields, height, columns,
        (incs, inc_above, inc_below, winds, above, below), (gathered,),
    )
    tail = row_count - halo
    f_above = jnp.stack([a[:, tail:] * x[:, tail:] - d[:, tail:] for a, x, d in zip(a_got, ends, d_got)])
    f_below = jnp.stack([a[:, :halo] * x[:, :halo] - d[:, :halo] for a, x, d in zip(a_got, ends, d_got)])
    f_above = lax.ppermute(f_above, "slab", [(i, i + 1) for i in range(slabs - 1)])
    f_below = lax.ppermute(f_below, "slab", [(i + 1, i) for i in range(slabs - 1)])
    dev = lax.dynamic_slice_in_dim(deviation, me * fields, fields, 1).transpose(1, 0, 2)
    scaled = sweep(
        adjoint_kernel, "adjoint", info, total_rows, (vertical, row_count, columns), fields, height, columns,
        (ends, f_above, f_below, dev, winds, above, below, *a_got, *d_got),
    )

    items = lax.all_to_all(scaled, "slab", split_axis=0, concat_axis=0, tiled=True)
    order = jnp.arange(slabs, dtype=jnp.int32) ^ slab
    place, bit, width = jnp.zeros_like(order), 1, slabs // 2
    while width:
        place = place + jnp.where((order & width) != 0, bit, 0)
        bit, width = bit * 2, width // 2
    variance = jnp.concatenate(
        [lax.dynamic_index_in_dim(bands, place[b], 0, keepdims=False) for b in range(slabs)]
    ).T
    filtered = covariance(items.reshape(total_rows, columns), variance)
    received = sent_home(filtered.reshape(slabs, row_count, columns), chain_len, slabs, fields)
    vmem = pl.BlockSpec(memory_space=pltpu.VMEM)
    gradient = pl.pallas_call(
        gradient_kernel,
        out_shape=jax.ShapeDtypeStruct(own.shape, jnp.float32),
        in_specs=[pl.BlockSpec(memory_space=pltpu.SMEM)] + [vmem] * (2 + vertical),
        out_specs=vmem,
        scratch_shapes=[pltpu.VMEM((vertical, row_count, columns), jnp.float32)],
        name="gradient",
    )(slab.reshape(1).astype(jnp.int32), own, deviation, *received)
    return gradient[None]


def solution(mesh):
    in_specs = (
        P("tm", "slab", None, None),
        P("tm", "slab", None, None),
        P("slab", None, None),
        P(None, "slab"),
        P("tm", "slab"),
        P("tm", "slab"),
        P("tm", "slab"),
    )
    out_specs = P("tm", "slab", None, None)
    return jax.shard_map(body, mesh=mesh, in_specs=in_specs, out_specs=out_specs, check_vma=False)
```
